1024 devices in a mesh: lev: 16 (over x_lo, y), lat: 64 (over z, x_hi, core).
Axes of the slice: x: 4 (x_hi: 2, x_lo: 2; x = x_hi * 2 + x_lo), y: 8, z: 16, core: 2. Of those that a mesh axis runs over, the one named last changes fastest.
Arguments:
- state: float32 [4, 128, 192, 1024], P(None, 'lev', 'lat'), may hold values from -6 to 6
- wind_east: float32 [128, 192, 1024], P('lev', 'lat'), may hold values from -0.45 to 0.45
- wind_north: float32 [128, 192, 1024], P('lev', 'lat'), may hold values from -0.45 to 0.45
- remap_weight: float32 [128, 128], replicated, may hold values from 0.05 to 1
- block_list: int32 [16, 64, 8], P('lev', 'lat'), may hold values from 0 to 7, as said below
- block_count: int32 [16, 64], P('lev', 'lat'), may hold values from 0 to 8, as said below
- w_in: bfloat16 [512, 1024], replicated, may hold values from -1 to 1
- w_mid: bfloat16 [1024, 1024], replicated, may hold values from -0.1875 to 0.1875
- w_out: bfloat16 [1024, 512], replicated, may hold values from -0.375 to 0.375
Outputs:
- new_state: float32 [4, 128, 192, 1024], P(None, 'lev', 'lat')
The draws below stay inside these ranges and needn't reach their ends.
Inputs may be any that keep to these rules, and one draw needn't show every extreme that they name: Each row block_list[m, g, :] names every block 0 to 7 exactly once. block_count[m, g] + block_count[m, (g + 32) mod 64] equals 8 for every m and g; some entry equals 8.
All inputs are finite; a program needn't handle non-finite values.
Results may differ from the reference program's by a relative error of at most 0.0045.
Values may be sent and summed in bfloat16 or wider, within the bound.
No kernel may reach another device: no remote copies, remote signals or barrier semaphores. Data moves between devices by JAX's collectives and lax.ppermute only.
A program may use at most 32 MiB of HBM per device.

```python
import math
import jax
import jax.numpy as jnp
from jax import lax

FIELDS = 4
L = 128
HID = 1024
NB = 8
NLON = 1024
D_IN = 512
NLAT = 192
BLK = 24
N_LEV = 16
N_LAT = 64


def draw_block_count(key, part):
    half_lat = N_LAT // 2
    base_counts = jax.random.randint(jax.random.fold_in(key, 11), (N_LEV, half_lat), 0, NB + 1)
    lev_pick = jax.random.randint(jax.random.fold_in(key, 12), (), 0, N_LEV)
    lat_pick = jax.random.randint(jax.random.fold_in(key, 13), (), 0, half_lat)
    extreme = jax.random.randint(jax.random.fold_in(key, 14), (), 0, 2) * NB
    lev_grid = lax.broadcasted_iota(jnp.int32, (N_LEV, half_lat), 0)
    lat_grid = lax.broadcasted_iota(jnp.int32, (N_LEV, half_lat), 1)
    chosen = (lev_grid == lev_pick) & (lat_grid == lat_pick)
    base_counts = jnp.where(chosen, extreme, base_counts)
    return jnp.concatenate([base_counts, NB - base_counts], axis=1).astype(jnp.int32)


def draw_block_list(key, part):
    subkeys = jax.random.split(jax.random.fold_in(key, 21), N_LEV * N_LAT)
    orders = jax.vmap(lambda subkey: jax.random.permutation(subkey, NB))(subkeys)
    return orders.reshape(N_LEV, N_LAT, NB).astype(jnp.int32)


def shard_levels(stream_key, dims, pieces, smallest, high):
    level, own = 1.0, jax.random.fold_in(stream_key, 6)
    for position, parts in pieces:
        draws = jnp.exp(jax.random.uniform(jax.random.fold_in(own, position), (parts,), jnp.float32, smallest / len(pieces), high / len(pieces)))
        level = level * jnp.repeat(draws, dims[position] // parts).reshape([-1 if axis == position else 1 for axis in range(len(dims))])
    return level


def scatter_about(rng, dims, spread, bound, cuts=(), kind=jnp.bfloat16):
    entries = spread * jax.random.normal(rng, dims, jnp.float32)
    if cuts:
        entries = entries * shard_levels(rng, dims, cuts, -0.22, 0.18)
    return jnp.clip(entries, -bound, bound).astype(kind)


def setup_inputs(seed: int = 0) -> dict:
    splits = jax.random.split(jax.random.key(seed), 10)
    state = scatter_about(splits[0], (FIELDS, L, NLAT, NLON), 1.0, 6.0, ((1, 16), (2, 64)), jnp.float32)
    wind_east = jnp.clip(jax.random.uniform(splits[1], (L, NLAT, NLON), jnp.float32, -0.45, 0.45) * shard_levels(splits[1], (L, NLAT, NLON), ((0, 16), (1, 64)), -0.4, 0.0), -0.45, 0.45)
    wind_north = jnp.clip(jax.random.uniform(splits[2], (L, NLAT, NLON), jnp.float32, -0.45, 0.45) * shard_levels(splits[2], (L, NLAT, NLON), ((0, 16), (1, 64)), -0.4, 0.0), -0.45, 0.45)
    remap_weight = jnp.clip(jnp.exp(jax.random.uniform(splits[3], (L, L), jnp.float32, math.log(0.05), math.log(1.0))), 0.05, 1.0)
    block_list = draw_block_list(jax.random.fold_in(splits[9], 71), 0)
    block_count = draw_block_count(jax.random.fold_in(splits[9], 71), 0)
    w_in = scatter_about(splits[6], (D_IN, HID), (D_IN // 16) ** -0.5, 1.0)
    w_mid = scatter_about(splits[7], (HID, HID), HID ** -0.5, 0.1875)
    w_out = scatter_about(splits[8], (HID, D_IN), (HID // 4) ** -0.5, 0.375)
    return dict(state=state, wind_east=wind_east, wind_north=wind_north, remap_weight=remap_weight, block_list=block_list, block_count=block_count, w_in=w_in, w_mid=w_mid, w_out=w_out)


def flux_update(state, wind_east, wind_north):
    global_row = lax.broadcasted_iota(jnp.int32, wind_north.shape, 1)
    northward = jnp.where(global_row == NLAT - 1, jnp.zeros_like(wind_north), wind_north)
    zeros_row = jnp.zeros_like(state[:, :, :1])
    north_cells = jnp.concatenate([state[:, :, 1:], zeros_row], axis=2)
    north_flux = jnp.maximum(northward, 0.0) * state + jnp.minimum(northward, 0.0) * north_cells
    south_flux = jnp.concatenate([zeros_row, north_flux[:, :, :-1]], axis=2)
    east_cells = jnp.roll(state, -1, axis=3)
    east_flux = jnp.maximum(wind_east, 0.0) * state + jnp.minimum(wind_east, 0.0) * east_cells
    west_flux = jnp.roll(east_flux, 1, axis=3)
    return state - (east_flux - west_flux) - (north_flux - south_flux)


def remap_matrix(remap_weight):
    identity = jnp.eye(remap_weight.shape[0], dtype=remap_weight.dtype)
    raw_weight = remap_weight + 16.0 * identity
    return raw_weight / jnp.sum(raw_weight, axis=1, keepdims=True)


def physics(inputs, w_in, w_mid, w_out):
    first = jax.nn.silu(jnp.dot(inputs, w_in, preferred_element_type=jnp.float32)).astype(jnp.bfloat16)
    second = jax.nn.silu(jnp.dot(first, w_mid, preferred_element_type=jnp.float32)).astype(jnp.bfloat16)
    return jnp.dot(second, w_out, preferred_element_type=jnp.float32)


def reference(state, wind_east, wind_north, remap_weight, block_list, block_count, w_in, w_mid, w_out):
    updated = flux_update(state, wind_east, wind_north)
    grouped = updated.reshape(FIELDS, L, N_LAT, N_LEV, NB, BLK)
    remapped = jnp.einsum('lk,fkgmbc->gmbcfl', remap_matrix(remap_weight), grouped, precision=lax.Precision.HIGHEST)
    columns = remapped.reshape(N_LAT, N_LEV, NB, BLK, FIELDS * L)
    half_lat = N_LAT // 2
    first_counts = block_count[:, :half_lat][:, :, None]
    slot_ids = lax.broadcasted_iota(jnp.int32, (N_LEV, half_lat, NB), 2)
    own_slot = slot_ids < first_counts
    other_slot = jnp.clip(slot_ids - first_counts, 0, NB - 1).astype(jnp.int32)
    other_list = jnp.take_along_axis(block_list[:, half_lat:], other_slot, axis=2)
    block_ids = jnp.where(own_slot, block_list[:, :half_lat], other_list).astype(jnp.int32).reshape(-1, NB)
    lat_base = lax.broadcasted_iota(jnp.int32, (N_LEV, half_lat, NB), 1)
    lat_ids = (lat_base + jnp.where(own_slot, 0, half_lat)).astype(jnp.int32).reshape(-1, NB)
    lev_ids = lax.broadcasted_iota(jnp.int32, (N_LEV, half_lat, NB), 0).reshape(-1, NB)

    def compute(index_sets):
        lat_set, lev_set, block_set = index_sets
        inputs = columns[lat_set, lev_set, block_set].astype(jnp.bfloat16).reshape(NB * BLK, FIELDS * L)
        return physics(inputs, w_in, w_mid, w_out).reshape(NB, BLK, FIELDS * L)

    tendency_blocks = lax.map(compute, (lat_ids, lev_ids, block_ids))
    tendency = jnp.zeros_like(columns).at[lat_ids, lev_ids, block_ids].set(tendency_blocks)
    finished = (columns + tendency).reshape(N_LAT, N_LEV, NB, BLK, FIELDS, L)
    return jnp.transpose(finished, (4, 5, 0, 1, 2, 3)).reshape(FIELDS, L, NLAT, NLON)
```

```python
import jax
import jax.numpy as jnp
from jax import lax
from jax.experimental import pallas as pl
from jax.experimental.pallas import tpu as pltpu
from jax.sharding import PartitionSpec as P

NB = 8
F32 = jnp.float32
BF16 = jnp.bfloat16
VM = pltpu.VMEM


def whole():
    return pl.BlockSpec(memory_space=VM)


def params(mib):
    return pltpu.CompilerParams(vmem_limit_bytes=mib * 2**20)


def edge_kernel(state_ref, north_ref, up_ref, down_ref):
    fields = state_ref.shape[0]
    for f in range(fields):
        up_ref[f] = state_ref[f, 2].astype(BF16)
        down_ref[f] = state_ref[f, 0].astype(BF16)
    up_ref[fields] = north_ref[2].astype(BF16)


def flux_kernel(state_ref, east_ref, north_ref, south_edge_ref, north_edge_ref, out_ref):
    fields, rows = state_ref.shape[:2]
    last = lax.axis_index("lat") == lax.axis_size("lat") - 1
    keep_wall = jnp.where(last, 0.0, 1.0).astype(F32)
    lane = lax.broadcasted_iota(jnp.int32, (8, 128), 1)
    low = lane < 64
    wind_below = south_edge_ref[fields].astype(F32)
    updated = []
    for f in range(fields):
        cells = [state_ref[f, j] for j in range(rows)]
        above = cells[1:] + [north_edge_ref[f].astype(F32)]
        below_flux = (
            jnp.maximum(wind_below, 0.0) * south_edge_ref[f].astype(F32)
            + jnp.minimum(wind_below, 0.0) * cells[0]
        )
        pieces = []
        for j in range(rows):
            wind = north_ref[j]
            if j == rows - 1:
                wind = wind * keep_wall
            north_flux = jnp.maximum(wind, 0.0) * cells[j] + jnp.minimum(wind, 0.0) * above[j]
            easterly = east_ref[j]
            width = cells[j].shape[1]
            east_cells = pltpu.roll(cells[j], width - 1, 1)
            east_flux = jnp.maximum(easterly, 0.0) * cells[j] + jnp.minimum(easterly, 0.0) * east_cells
            west_flux = pltpu.roll(east_flux, 1, 1)
            pieces.append(cells[j] - (east_flux - west_flux) - (north_flux - below_flux))
            below_flux = north_flux
        updated.append(pieces)

    def tile(f, v):
        j, k = divmod(v, 8)
        return updated[f][j][:, k * 128 : (k + 1) * 128]

    for p in range(8):
        full_a = [tile(f, 3 * p) for f in range(fields)]
        half = [tile(f, 3 * p + 1) for f in range(fields)]
        full_b = [tile(f, 3 * p + 2) for f in range(fields)]
        turned = [pltpu.roll(h, 64, 1) for h in half]
        half_a = [jnp.where(low, half[f], turned[f + 2]) for f in range(2)]
        half_b = [jnp.where(low, turned[f], half[f + 2]) for f in range(2)]
        out_ref[2 * p] = jnp.concatenate(full_a + half_a, axis=0).astype(BF16)
        out_ref[2 * p + 1] = jnp.concatenate(full_b + half_b, axis=0).astype(BF16)


def remap_kernel(weight_ref, high_ref, low_ref):
    n = weight_ref.shape[0]
    row = lax.broadcasted_iota(jnp.int32, (n, n), 0)
    col = lax.broadcasted_iota(jnp.int32, (n, n), 1)
    raw = weight_ref[...] + jnp.where(row == col, 16.0, 0.0)
    remap = (raw / jnp.sum(raw, axis=1, keepdims=True)).T
    zero = jnp.zeros((8, n), F32)
    rows = []
    for m in range(n // 8):
        piece = remap[m * 8 : (m + 1) * 8]
        rows.append(jnp.concatenate([piece, zero], axis=1))
        rows.append(jnp.concatenate([zero, piece], axis=1))
    pair = jnp.concatenate(rows, axis=0)
    high = pair.astype(BF16)
    high_ref[...] = high
    low_ref[...] = (pair - high.astype(F32)).astype(BF16)


def silu(v):
    return v / (1.0 + jnp.exp(-v))


def physics_kernel(list_ref, count_ref, data_ref, high_ref, low_ref, w_in_ref, w_mid_ref, w_out_ref, out_ref):
    bits = jnp.int32(0)
    count = count_ref[0, 0]
    for s in range(NB):
        bits = bits + jnp.where(s < count, jnp.left_shift(jnp.int32(1), list_ref[0, 0, s]), 0)
    odd = lax.rem(lax.axis_index("lev"), 2)

    def turned(r):
        block = data_ref[:, r : r + 16, :].reshape(256, 128)
        return block.T

    ends = turned(32)
    x = []
    for p in range(2):
        cols = jnp.concatenate([turned(16 * p), ends[64 * p : 64 * p + 64]], axis=0)
        x.append(
            jnp.dot(cols, high_ref[...], preferred_element_type=F32)
            + jnp.dot(cols, low_ref[...], preferred_element_type=F32)
        )
    remapped = jnp.concatenate(x, axis=1)
    first = silu(jnp.dot(remapped.astype(BF16), w_in_ref[...], preferred_element_type=F32)).astype(BF16)
    second = silu(jnp.dot(first, w_mid_ref[...], preferred_element_type=F32)).astype(BF16)
    tendency = jnp.dot(second, w_out_ref[...], preferred_element_type=F32)
    place = lax.broadcasted_iota(jnp.int32, tendency.shape, 0)
    column = jnp.where(place < 128, place + 64 * odd, place - 128 * odd)
    block = jnp.right_shift(column * 2731, 16)
    active = jnp.bitwise_and(jnp.right_shift(jnp.full(tendency.shape, bits), block), 1) == 1
    finished = remapped + jnp.where(active, tendency, 0.0)

    def put(r, rows):
        back = rows.T.reshape(2, 16, 8, 128)
        both = jnp.concatenate([back[0], back[1]], axis=1)
        out_ref[:, r : r + 16, :] = both.astype(BF16)

    put(0, finished[:128, :256])
    put(16, finished[:128, 256:])
    put(32, jnp.concatenate([finished[128:, :256], finished[128:, 256:]], axis=0))


def unpack_kernel(data_ref, out_ref):
    fields = out_ref.shape[0]
    lane = lax.broadcasted_iota(jnp.int32, (16, 128), 1)
    low = lane < 64

    def put(v, pair, value):
        j, k = divmod(v, 8)
        for f in range(2):
            out_ref[2 * pair + f, j, :, k * 128 : (k + 1) * 128] = value[8 * f : 8 * f + 8]

    for p in range(8):
        a = data_ref[2 * p].astype(F32)
        b = data_ref[2 * p + 1].astype(F32)
        for pair in range(2):
            put(3 * p, pair, a[16 * pair : 16 * pair + 16])
            put(3 * p + 2, pair, b[16 * pair : 16 * pair + 16])
        end_a, end_b = a[32:], b[32:]
        put(3 * p + 1, 0, jnp.where(low, end_a, pltpu.roll(end_b, 64, 1)))
        put(3 * p + 1, 1, jnp.where(low, pltpu.roll(end_a, 64, 1), end_b))


def per_device(
    state, wind_east, wind_north, remap_weight, block_list, block_count, w_in, w_mid, w_out
):
    fields, lev_dev, lat_rows, lon_cells = state.shape
    lev_count = lax.axis_size("lev")
    lat_count = lax.axis_size("lat")
    cells = jnp.transpose(state, (0, 2, 1, 3))
    east = jnp.transpose(wind_east, (1, 0, 2))
    north = jnp.transpose(wind_north, (1, 0, 2))
    edge = (lev_dev, lon_cells)
    up, down = pl.pallas_call(
        edge_kernel,
        out_shape=[
            jax.ShapeDtypeStruct((fields + 1, *edge), BF16),
            jax.ShapeDtypeStruct((fields, *edge), BF16),
        ],
        in_specs=[whole()] * 2,
        out_specs=[whole()] * 2,
        compiler_params=params(8),
        name="edges",
    )(cells, north)
    south_edge = lax.ppermute(up, "lat", [(i, i + 1) for i in range(lat_count - 1)])
    north_edge = lax.ppermute(down, "lat", [(i + 1, i) for i in range(lat_count - 1)])
    chunk = (lev_count, fields * lev_dev * lat_rows * lon_cells // lev_count // 128, 128)
    packed = pl.pallas_call(
        flux_kernel,
        out_shape=jax.ShapeDtypeStruct(chunk, BF16),
        in_specs=[whole()] * 5,
        out_specs=whole(),
        compiler_params=params(8),
        name="flux",
    )(cells, east, north, south_edge, north_edge)
    levels = lev_dev * lev_count
    high, low = pl.pallas_call(
        remap_kernel,
        out_shape=[jax.ShapeDtypeStruct((2 * levels, 2 * levels), BF16)] * 2,
        in_specs=[whole()],
        out_specs=[whole()] * 2,
        compiler_params=params(8),
        name="remap",
    )(remap_weight)
    columns = lax.all_to_all(packed, "lev", split_axis=0, concat_axis=0, tiled=True)
    smem = pl.BlockSpec(memory_space=pltpu.SMEM)
    finished = pl.pallas_call(
        physics_kernel,
        out_shape=jax.ShapeDtypeStruct(chunk, BF16),
        in_specs=[smem, smem] + [whole()] * 6,
        out_specs=whole(),
        compiler_params=params(24),
        name="physics",
    )(block_list, block_count, columns, high, low, w_in, w_mid, w_out)
    returned = lax.all_to_all(finished, "lev", split_axis=0, concat_axis=0, tiled=True)
    result = pl.pallas_call(
        unpack_kernel,
        out_shape=jax.ShapeDtypeStruct(cells.shape, F32),
        in_specs=[whole()],
        out_specs=whole(),
        compiler_params=params(8),
        name="unpack",
    )(returned)
    return jnp.transpose(result, (0, 2, 1, 3))


def solution(mesh):
    placed = (
        P(None, "lev", "lat", None),
        P("lev", "lat", None),
        P("lev", "lat", None),
        P(),
        P("lev", "lat", None),
        P("lev", "lat"),
        P(),
        P(),
        P(),
    )
    return jax.shard_map(
        per_device,
        mesh=mesh,
        in_specs=placed,
        out_specs=P(None, "lev", "lat", None),
        check_vma=False,
    )
```

```python
import jax
import jax.numpy as jnp
from jax import lax
from jax.experimental import pallas as pl
from jax.experimental.pallas import tpu as pltpu
from jax.sharding import PartitionSpec as P

NB = 8
F32 = jnp.float32
BF16 = jnp.bfloat16
VM = pltpu.VMEM


def whole():
    return pl.BlockSpec(memory_space=VM)


def in_hbm(array):
    return pltpu.with_memory_space_constraint(array, pltpu.HBM)


def cost(flops, moved):
    return pl.CostEstimate(flops=flops, bytes_accessed=moved, transcendentals=0)


def params(mib):
    return pltpu.CompilerParams(vmem_limit_bytes=mib * 2**20)


def load_kernel(state_ref, east_ref, north_ref, cells_ref, easterly_ref, northerly_ref, up_ref, down_ref, sems):
    fields, rows = state_ref.shape[:2]
    last = rows - 1

    def bring(source, target, k):
        copy = pltpu.make_async_copy(source, target, sems.at[k])
        copy.start()
        return copy

    first = [
        bring(state_ref.at[:, last], cells_ref.at[:, last], 0),
        bring(north_ref.at[last], northerly_ref.at[last], 1),
        bring(state_ref.at[:, 0], cells_ref.at[:, 0], 2),
    ]
    rest = [
        bring(state_ref.at[:, 1:last], cells_ref.at[:, 1:last], 3),
        bring(north_ref.at[:last], northerly_ref.at[:last], 4),
        bring(east_ref, easterly_ref, 5),
    ]
    for copy in first:
        copy.wait()
    for f in range(fields):
        up_ref[f] = cells_ref[f, last].astype(BF16)
        down_ref[f] = cells_ref[f, 0].astype(BF16)
    up_ref[fields] = northerly_ref[last].astype(BF16)
    for copy in rest:
        copy.wait()


def pair_remap(weight):
    n = weight.shape[0]
    row = lax.broadcasted_iota(jnp.int32, (n, n), 0)
    col = lax.broadcasted_iota(jnp.int32, (n, n), 1)
    raw = weight + jnp.where(row == col, 16.0, 0.0)
    remap = (raw / jnp.sum(raw, axis=1, keepdims=True)).T
    zero = jnp.zeros((8, n), F32)
    rows = []
    for m in range(n // 8):
        piece = remap[m * 8 : (m + 1) * 8]
        rows.append(jnp.concatenate([piece, zero], axis=1))
        rows.append(jnp.concatenate([zero, piece], axis=1))
    return jnp.concatenate(rows, axis=0)


def local_kernel(
    state_ref, east_ref, north_ref, list_ref, count_ref, weight_ref, w_in_ref, w_mid_ref,
    out_ref, high_ref, low_ref, mask_ref, w_in_out, w_mid_out, order, weight, sems,
):
    copies = [
        pltpu.make_async_copy(source, target, sems.at[k])
        for k, (source, target) in enumerate(
            ((list_ref, order), (weight_ref, weight), (w_in_ref, w_in_out), (w_mid_ref, w_mid_out))
        )
    ]
    for copy in copies:
        copy.start()
    fields, rows, _, width = state_ref.shape
    for f in range(fields):
        below_flux = None
        for j in range(rows):
            cells = state_ref[f, j]
            wind = north_ref[j]
            easterly = east_ref[j]
            east_cells = pltpu.roll(cells, width - 1, 1)
            east_flux = jnp.maximum(easterly, 0.0) * cells + jnp.minimum(easterly, 0.0) * east_cells
            west_flux = pltpu.roll(east_flux, 1, 1)
            value = cells - (east_flux - west_flux)
            if below_flux is not None:
                value = value + below_flux
            if j < rows - 1:
                below_flux = jnp.maximum(wind, 0.0) * cells + jnp.minimum(wind, 0.0) * state_ref[f, j + 1]
                value = value - below_flux
            out_ref[f, j] = value
    for copy in copies[:2]:
        copy.wait()
    pair = pair_remap(weight[...])
    high = pair.astype(BF16)
    high_ref[...] = high
    low_ref[...] = (pair - high.astype(F32)).astype(BF16)
    bits = jnp.int32(0)
    count = count_ref[0, 0]
    for s in range(NB):
        bits = bits + jnp.where(s < count, jnp.left_shift(jnp.int32(1), order[0, 0, s]), 0)
    odd = lax.rem(lax.axis_index("lev"), 2)
    place = lax.broadcasted_iota(jnp.int32, mask_ref.shape, 0)
    column = jnp.where(place < 128, place + 64 * odd, place - 128 * odd)
    block = jnp.right_shift(column * 2731, 16)
    active = jnp.bitwise_and(jnp.right_shift(jnp.full(mask_ref.shape, bits), block), 1)
    mask_ref[...] = active.astype(F32)
    for copy in copies[2:]:
        copy.wait()


def finish_kernel(local_ref, state_ref, north_ref, south_edge_ref, north_edge_ref, out_ref):
    fields, rows = state_ref.shape[:2]
    last = rows - 1
    wall = lax.axis_index("lat") == lax.axis_size("lat") - 1
    wind = north_ref[last] * jnp.where(wall, 0.0, 1.0).astype(F32)
    wind_below = south_edge_ref[fields].astype(F32)
    rising, sinking = jnp.maximum(wind, 0.0), jnp.minimum(wind, 0.0)
    rising_below, sinking_below = jnp.maximum(wind_below, 0.0), jnp.minimum(wind_below, 0.0)
    low = lax.broadcasted_iota(jnp.int32, (8, 128), 1) < 64
    updated = []
    for f in range(fields):
        south = rising_below * south_edge_ref[f].astype(F32) + sinking_below * state_ref[f, 0]
        north = rising * state_ref[f, last] + sinking * north_edge_ref[f].astype(F32)
        pieces = [local_ref[f, j] for j in range(rows)]
        pieces[0] = pieces[0] + south
        pieces[last] = pieces[last] - north
        updated.append(pieces)

    def tile(f, v):
        j, k = divmod(v, 8)
        return updated[f][j][:, k * 128 : (k + 1) * 128]

    for p in range(8):
        full_a = [tile(f, 3 * p) for f in range(fields)]
        half = [tile(f, 3 * p + 1) for f in range(fields)]
        full_b = [tile(f, 3 * p + 2) for f in range(fields)]
        turned = [pltpu.roll(h, 64, 1) for h in half]
        half_a = [jnp.where(low, half[f], turned[f + 2]) for f in range(2)]
        half_b = [jnp.where(low, turned[f], half[f + 2]) for f in range(2)]
        out_ref[2 * p] = jnp.concatenate(full_a + half_a, axis=0).astype(BF16)
        out_ref[2 * p + 1] = jnp.concatenate(full_b + half_b, axis=0).astype(BF16)


def silu(v):
    return v / (1.0 + jnp.exp(-v))


def physics_kernel(
    data_ref, high_ref, low_ref, mask_ref, w_in_ref, w_mid_ref, w_out_ref, out_ref, w_out, sem
):
    last_layer = pltpu.make_async_copy(w_out_ref, w_out, sem)
    last_layer.start()

    def turned(r):
        block = data_ref[:, r : r + 16, :].reshape(256, 128)
        return block.T

    ends = turned(32)
    x = []
    for p in range(2):
        cols = jnp.concatenate([turned(16 * p), ends[64 * p : 64 * p + 64]], axis=0)
        x.append(
            jnp.dot(cols, high_ref[...], preferred_element_type=F32)
            + jnp.dot(cols, low_ref[...], preferred_element_type=F32)
        )
    remapped = jnp.concatenate(x, axis=1)
    first = silu(jnp.dot(remapped.astype(BF16), w_in_ref[...], preferred_element_type=F32)).astype(BF16)
    second = silu(jnp.dot(first, w_mid_ref[...], preferred_element_type=F32)).astype(BF16)
    last_layer.wait()
    tendency = jnp.dot(second, w_out[...], preferred_element_type=F32)
    active = jnp.concatenate([mask_ref[...]] * 4, axis=1) > 0.0
    finished = remapped + jnp.where(active, tendency, 0.0)

    def put(r, rows):
        back = rows.T.reshape(2, 16, 8, 128)
        both = jnp.concatenate([back[0], back[1]], axis=1)
        out_ref[:, r : r + 16, :] = both.astype(BF16)

    put(0, finished[:128, :256])
    put(16, finished[:128, 256:])
    put(32, jnp.concatenate([finished[128:, :256], finished[128:, 256:]], axis=0))


def unpack_kernel(data_ref, out_ref):
    fields = out_ref.shape[0]
    lane = lax.broadcasted_iota(jnp.int32, (16, 128), 1)
    low = lane < 64

    def put(v, pair, value):
        j, k = divmod(v, 8)
        for f in range(2):
            out_ref[2 * pair + f, j, :, k * 128 : (k + 1) * 128] = value[8 * f : 8 * f + 8]

    for p in range(8):
        a = data_ref[2 * p].astype(F32)
        b = data_ref[2 * p + 1].astype(F32)
        for pair in range(2):
            put(3 * p, pair, a[16 * pair : 16 * pair + 16])
            put(3 * p + 2, pair, b[16 * pair : 16 * pair + 16])
        end_a, end_b = a[32:], b[32:]
        put(3 * p + 1, 0, jnp.where(low, end_a, pltpu.roll(end_b, 64, 1)))
        put(3 * p + 1, 1, jnp.where(low, pltpu.roll(end_a, 64, 1), end_b))


def per_device(
    state, wind_east, wind_north, remap_weight, block_list, block_count, w_in, w_mid, w_out
):
    fields, lev_dev, lat_rows, lon_cells = state.shape
    lev_count = lax.axis_size("lev")
    lat_count = lax.axis_size("lat")
    cells = jnp.transpose(state, (0, 2, 1, 3))
    east = jnp.transpose(wind_east, (1, 0, 2))
    north = jnp.transpose(wind_north, (1, 0, 2))
    edge = (lev_dev, lon_cells)
    smem = pl.BlockSpec(memory_space=pltpu.SMEM)
    hbm = pl.BlockSpec(memory_space=pltpu.HBM)
    levels = lev_dev * lev_count
    col_count = lat_rows * lon_cells // lev_count
    held_cells, held_east, held_north, up, down = pl.pallas_call(
        load_kernel,
        out_shape=[
            jax.ShapeDtypeStruct(cells.shape, F32),
            jax.ShapeDtypeStruct(east.shape, F32),
            jax.ShapeDtypeStruct(north.shape, F32),
            jax.ShapeDtypeStruct((fields + 1, *edge), BF16),
            jax.ShapeDtypeStruct((fields, *edge), BF16),
        ],
        in_specs=[hbm] * 3,
        out_specs=[whole()] * 5,
        scratch_shapes=[pltpu.SemaphoreType.DMA((6,))],
        compiler_params=params(4),
        cost_estimate=cost(1 << 17, 1 << 21),
        name="load",
    )(*map(in_hbm, (cells, east, north)))
    south_edge = lax.ppermute(up, "lat", [(i, i + 1) for i in range(lat_count - 1)])
    north_edge = lax.ppermute(down, "lat", [(i + 1, i) for i in range(lat_count - 1)])
    local, high, low, mask, held_in, held_mid = pl.pallas_call(
        local_kernel,
        out_shape=[
            jax.ShapeDtypeStruct(cells.shape, F32),
            jax.ShapeDtypeStruct((2 * levels, 2 * levels), BF16),
            jax.ShapeDtypeStruct((2 * levels, 2 * levels), BF16),
            jax.ShapeDtypeStruct((col_count, 128), F32),
            jax.ShapeDtypeStruct(w_in.shape, BF16),
            jax.ShapeDtypeStruct(w_mid.shape, BF16),
        ],
        in_specs=[whole()] * 3 + [hbm, smem] + [hbm] * 3,
        out_specs=[whole()] * 6,
        scratch_shapes=[
            pltpu.SMEM(block_list.shape, jnp.int32),
            VM(remap_weight.shape, F32),
            pltpu.SemaphoreType.DMA((4,)),
        ],
        compiler_params=params(4),
        cost_estimate=cost(1 << 22, 1 << 22),
        name="local",
    )(held_cells, held_east, held_north, in_hbm(block_list), block_count, *map(in_hbm, (remap_weight, w_in, w_mid)))
    chunk = (lev_count, fields * lev_dev * lat_rows * lon_cells // lev_count // 128, 128)
    packed = pl.pallas_call(
        finish_kernel,
        out_shape=jax.ShapeDtypeStruct(chunk, BF16),
        in_specs=[whole()] * 5,
        out_specs=whole(),
        compiler_params=params(4),
        cost_estimate=cost(1 << 20, 1 << 20),
        name="finish",
    )(local, held_cells, held_north, south_edge, north_edge)
    packed, high, low, mask, held_in, held_mid = lax.optimization_barrier(
        (packed, high, low, mask, held_in, held_mid)
    )
    columns = lax.all_to_all(packed, "lev", split_axis=0, concat_axis=0, tiled=True)
    finished = pl.pallas_call(
        physics_kernel,
        out_shape=jax.ShapeDtypeStruct(chunk, BF16),
        in_specs=[whole()] * 6 + [hbm],
        out_specs=whole(),
        scratch_shapes=[VM(w_out.shape, BF16), pltpu.SemaphoreType.DMA(())],
        compiler_params=params(16),
        cost_estimate=cost(1 << 30, 1 << 22),
        name="physics",
    )(columns, high, low, mask, held_in, held_mid, in_hbm(w_out))
    returned = lax.all_to_all(finished, "lev", split_axis=0, concat_axis=0, tiled=True)
    result = pl.pallas_call(
        unpack_kernel,
        out_shape=jax.ShapeDtypeStruct(cells.shape, F32),
        in_specs=[whole()],
        out_specs=whole(),
        compiler_params=params(4),
        cost_estimate=cost(1 << 18, 1 << 20),
        name="unpack",
    )(returned)
    return jnp.transpose(result, (0, 2, 1, 3))


def solution(mesh):
    placed = (
        P(None, "lev", "lat", None),
        P("lev", "lat", None),
        P("lev", "lat", None),
        P(),
        P("lev", "lat", None),
        P("lev", "lat"),
        P(),
        P(),
        P(),
    )
    return jax.shard_map(
        per_device,
        mesh=mesh,
        in_specs=placed,
        out_specs=P(None, "lev", "lat", None),
        check_vma=False,
    )
```

```python
import jax
import jax.numpy as jnp
from jax import lax
from jax.experimental import pallas as pl
from jax.experimental.pallas import tpu as pltpu
from jax.sharding import PartitionSpec as P

NB = 8
F32 = jnp.float32
BF16 = jnp.bfloat16
VM = pltpu.VMEM


def whole():
    return pl.BlockSpec(memory_space=VM)


def in_hbm(array):
    return pltpu.with_memory_space_constraint(array, pltpu.HBM)


def cost(flops, moved):
    return pl.CostEstimate(flops=flops, bytes_accessed=moved, transcendentals=0)


def params(mib):
    return pltpu.CompilerParams(vmem_limit_bytes=mib * 2**20)


def even_band():
    return lax.rem(lax.axis_index("lat"), 2) == 0


def load_kernel(state_ref, east_ref, north_ref, cells_ref, easterly_ref, northerly_ref, near_ref, far_ref, sems):
    fields, rows = state_ref.shape[:2]
    last = rows - 1

    def bring(source, target, k):
        copy = pltpu.make_async_copy(source, target, sems.at[k])
        copy.start()
        return copy

    first = [
        bring(state_ref.at[:, last], cells_ref.at[:, last], 0),
        bring(north_ref.at[last], northerly_ref.at[last], 1),
        bring(state_ref.at[:, 0], cells_ref.at[:, 0], 2),
        bring(north_ref.at[:last], northerly_ref.at[:last], 4),
    ]
    rest = [
        bring(state_ref.at[:, 1:last], cells_ref.at[:, 1:last], 3),
        bring(east_ref, easterly_ref, 5),
    ]
    for copy in first:
        copy.wait()
    near_row = jnp.where(even_band(), last, 0)
    for edge_ref, row in ((near_ref, near_row), (far_ref, last - near_row)):
        for f in range(fields):
            edge_ref[f] = cells_ref[f, row].astype(BF16)
        edge_ref[fields] = northerly_ref[row].astype(BF16)
    for copy in rest:
        copy.wait()


def pair_remap(weight):
    n = weight.shape[0]
    row = lax.broadcasted_iota(jnp.int32, (n, n), 0)
    col = lax.broadcasted_iota(jnp.int32, (n, n), 1)
    raw = weight + jnp.where(row == col, 16.0, 0.0)
    remap = (raw / jnp.sum(raw, axis=1, keepdims=True)).T
    zero = jnp.zeros((8, n), F32)
    rows = []
    for m in range(n // 8):
        piece = remap[m * 8 : (m + 1) * 8]
        rows.append(jnp.concatenate([piece, zero], axis=1))
        rows.append(jnp.concatenate([zero, piece], axis=1))
    return jnp.concatenate(rows, axis=0)


def local_kernel(
    state_ref, east_ref, north_ref, list_ref, count_ref, weight_ref,
    out_ref, high_ref, low_ref, mask_ref, order, weight, sems,
):
    copies = [
        pltpu.make_async_copy(source, target, sems.at[k])
        for k, (source, target) in enumerate(
            ((list_ref, order), (weight_ref, weight))
        )
    ]
    for copy in copies:
        copy.start()
    fields, rows, _, width = state_ref.shape
    for f in range(fields):
        below_flux = None
        for j in range(rows):
            cells = state_ref[f, j]
            wind = north_ref[j]
            easterly = east_ref[j]
            east_cells = pltpu.roll(cells, width - 1, 1)
            east_flux = jnp.maximum(easterly, 0.0) * cells + jnp.minimum(easterly, 0.0) * east_cells
            west_flux = pltpu.roll(east_flux, 1, 1)
            value = cells - (east_flux - west_flux)
            if below_flux is not None:
                value = value + below_flux
            if j < rows - 1:
                below_flux = jnp.maximum(wind, 0.0) * cells + jnp.minimum(wind, 0.0) * state_ref[f, j + 1]
                value = value - below_flux
            out_ref[f, j] = value
    for copy in copies:
        copy.wait()
    pair = pair_remap(weight[...])
    high = pair.astype(BF16)
    high_ref[...] = high
    low_ref[...] = (pair - high.astype(F32)).astype(BF16)
    bits = jnp.int32(0)
    count = count_ref[0, 0]
    for s in range(NB):
        bits = bits + jnp.where(s < count, jnp.left_shift(jnp.int32(1), order[0, 0, s]), 0)
    odd = lax.rem(lax.axis_index("lev"), 2)
    place = lax.broadcasted_iota(jnp.int32, mask_ref.shape, 0)
    column = jnp.where(place < 128, place + 64 * odd, place - 128 * odd)
    block = jnp.right_shift(column * 2731, 16)
    active = jnp.bitwise_and(jnp.right_shift(jnp.full(mask_ref.shape, bits), block), 1)
    mask_ref[...] = active.astype(F32)


def finish_kernel(local_ref, state_ref, north_ref, near_ref, far_ref, out_ref):
    fields, rows = state_ref.shape[:2]
    last = rows - 1
    wall = lax.axis_index("lat") == lax.axis_size("lat") - 1
    wind = north_ref[last] * jnp.where(wall, 0.0, 1.0).astype(F32)
    even = even_band()

    def edge(first, second, f):
        return jnp.where(even, first[f].astype(F32), second[f].astype(F32))

    wind_below = edge(far_ref, near_ref, fields)
    rising, sinking = jnp.maximum(wind, 0.0), jnp.minimum(wind, 0.0)
    rising_below, sinking_below = jnp.maximum(wind_below, 0.0), jnp.minimum(wind_below, 0.0)
    low = lax.broadcasted_iota(jnp.int32, (8, 128), 1) < 64
    updated = []
    for f in range(fields):
        south = rising_below * edge(far_ref, near_ref, f) + sinking_below * state_ref[f, 0]
        north = rising * state_ref[f, last] + sinking * edge(near_ref, far_ref, f)
        pieces = [local_ref[f, j] for j in range(rows)]
        pieces[0] = pieces[0] + south
        pieces[last] = pieces[last] - north
        updated.append(pieces)

    def tile(f, v):
        j, k = divmod(v, 8)
        return updated[f][j][:, k * 128 : (k + 1) * 128]

    for p in range(8):
        full_a = [tile(f, 3 * p) for f in range(fields)]
        half = [tile(f, 3 * p + 1) for f in range(fields)]
        full_b = [tile(f, 3 * p + 2) for f in range(fields)]
        turned = [pltpu.roll(h, 64, 1) for h in half]
        half_a = [jnp.where(low, half[f], turned[f + 2]) for f in range(2)]
        half_b = [jnp.where(low, turned[f], half[f + 2]) for f in range(2)]
        out_ref[2 * p] = jnp.concatenate(full_a + half_a, axis=0).astype(BF16)
        out_ref[2 * p + 1] = jnp.concatenate(full_b + half_b, axis=0).astype(BF16)


def silu(v):
    return v / (1.0 + jnp.exp(-v))


def physics_kernel(
    data_ref, high_ref, low_ref, mask_ref, w_in_ref, w_mid_ref, w_out_ref, out_ref
):
    def turned(r):
        block = data_ref[:, r : r + 16, :].reshape(256, 128)
        return block.T

    ends = turned(32)
    x = []
    for p in range(2):
        cols = jnp.concatenate([turned(16 * p), ends[64 * p : 64 * p + 64]], axis=0)
        x.append(
            jnp.dot(cols, high_ref[...], preferred_element_type=F32)
            + jnp.dot(cols, low_ref[...], preferred_element_type=F32)
        )
    remapped = jnp.concatenate(x, axis=1)
    first = silu(jnp.dot(remapped.astype(BF16), w_in_ref[...], preferred_element_type=F32)).astype(BF16)
    second = silu(jnp.dot(first, w_mid_ref[...], preferred_element_type=F32)).astype(BF16)
    tendency = jnp.dot(second, w_out_ref[...], preferred_element_type=F32)
    active = jnp.concatenate([mask_ref[...]] * 4, axis=1) > 0.0
    finished = remapped + jnp.where(active, tendency, 0.0)

    def put(r, rows):
        back = rows.T.reshape(2, 16, 8, 128)
        both = jnp.concatenate([back[0], back[1]], axis=1)
        out_ref[:, r : r + 16, :] = both.astype(BF16)

    put(0, finished[:128, :256])
    put(16, finished[:128, 256:])
    put(32, jnp.concatenate([finished[128:, :256], finished[128:, 256:]], axis=0))


def unpack_kernel(data_ref, out_ref):
    fields = out_ref.shape[0]
    lane = lax.broadcasted_iota(jnp.int32, (16, 128), 1)
    low = lane < 64

    def put(v, pair, value):
        j, k = divmod(v, 8)
        for f in range(2):
            out_ref[2 * pair + f, j, :, k * 128 : (k + 1) * 128] = value[8 * f : 8 * f + 8]

    for p in range(8):
        a = data_ref[2 * p].astype(F32)
        b = data_ref[2 * p + 1].astype(F32)
        for pair in range(2):
            put(3 * p, pair, a[16 * pair : 16 * pair + 16])
            put(3 * p + 2, pair, b[16 * pair : 16 * pair + 16])
        end_a, end_b = a[32:], b[32:]
        put(3 * p + 1, 0, jnp.where(low, end_a, pltpu.roll(end_b, 64, 1)))
        put(3 * p + 1, 1, jnp.where(low, pltpu.roll(end_a, 64, 1), end_b))


def pairs(start, count):
    lower = range(start, count - 1, 2)
    return [(i, i + 1) for i in lower] + [(i + 1, i) for i in lower]


def per_device(
    state, wind_east, wind_north, remap_weight, block_list, block_count, w_in, w_mid, w_out
):
    fields, lev_dev, lat_rows, lon_cells = state.shape
    lev_count = lax.axis_size("lev")
    lat_count = lax.axis_size("lat")
    cells = jnp.transpose(state, (0, 2, 1, 3))
    east = jnp.transpose(wind_east, (1, 0, 2))
    north = jnp.transpose(wind_north, (1, 0, 2))
    edge = (lev_dev, lon_cells)
    smem = pl.BlockSpec(memory_space=pltpu.SMEM)
    hbm = pl.BlockSpec(memory_space=pltpu.HBM)
    levels = lev_dev * lev_count
    col_count = lat_rows * lon_cells // lev_count
    held_cells, held_east, held_north, near, far = pl.pallas_call(
        load_kernel,
        out_shape=[
            jax.ShapeDtypeStruct(cells.shape, F32),
            jax.ShapeDtypeStruct(east.shape, F32),
            jax.ShapeDtypeStruct(north.shape, F32),
            jax.ShapeDtypeStruct((fields + 1, *edge), BF16),
            jax.ShapeDtypeStruct((fields + 1, *edge), BF16),
        ],
        in_specs=[hbm] * 3,
        out_specs=[whole()] * 5,
        scratch_shapes=[pltpu.SemaphoreType.DMA((6,))],
        compiler_params=params(4),
        cost_estimate=cost(1 << 17, 1 << 21),
        name="load",
    )(*map(in_hbm, (cells, east, north)))
    far = lax.ppermute(far, "lat", pairs(1, lat_count))
    near = lax.ppermute(near, "lat", pairs(0, lat_count))
    local, high, low, mask = pl.pallas_call(
        local_kernel,
        out_shape=[
            jax.ShapeDtypeStruct(cells.shape, F32),
            jax.ShapeDtypeStruct((2 * levels, 2 * levels), BF16),
            jax.ShapeDtypeStruct((2 * levels, 2 * levels), BF16),
            jax.ShapeDtypeStruct((col_count, 128), F32),
        ],
        in_specs=[whole()] * 3 + [hbm, smem, hbm],
        out_specs=[whole()] * 4,
        scratch_shapes=[
            pltpu.SMEM(block_list.shape, jnp.int32),
            VM(remap_weight.shape, F32),
            pltpu.SemaphoreType.DMA((2,)),
        ],
        compiler_params=params(4),
        cost_estimate=cost(1 << 22, 1 << 22),
        name="local",
    )(held_cells, held_east, held_north, in_hbm(block_list), block_count, in_hbm(remap_weight))
    chunk = (lev_count, fields * lev_dev * lat_rows * lon_cells // lev_count // 128, 128)
    packed = pl.pallas_call(
        finish_kernel,
        out_shape=jax.ShapeDtypeStruct(chunk, BF16),
        in_specs=[whole()] * 5,
        out_specs=whole(),
        compiler_params=params(4),
        cost_estimate=cost(1 << 34, 1 << 20),
        name="finish",
    )(local, held_cells, held_north, near, far)
    packed, high, low, mask = lax.optimization_barrier((packed, high, low, mask))
    columns = lax.all_to_all(packed, "lev", split_axis=0, concat_axis=0, tiled=True)
    finished = pl.pallas_call(
        physics_kernel,
        out_shape=jax.ShapeDtypeStruct(chunk, BF16),
        in_specs=[whole()] * 7,
        out_specs=whole(),
        compiler_params=params(16),
        cost_estimate=cost(1 << 30, 1 << 22),
        name="physics",
    )(columns, high, low, mask, w_in, w_mid, w_out)
    returned = lax.all_to_all(finished, "lev", split_axis=0, concat_axis=0, tiled=True)
    result = pl.pallas_call(
        unpack_kernel,
        out_shape=jax.ShapeDtypeStruct(cells.shape, F32),
        in_specs=[whole()],
        out_specs=whole(),
        compiler_params=params(4),
        cost_estimate=cost(1 << 18, 1 << 20),
        name="unpack",
    )(returned)
    return jnp.transpose(result, (0, 2, 1, 3))


def solution(mesh):
    placed = (
        P(None, "lev", "lat", None),
        P("lev", "lat", None),
        P("lev", "lat", None),
        P(),
        P("lev", "lat", None),
        P("lev", "lat"),
        P(),
        P(),
        P(),
    )
    return jax.shard_map(
        per_device,
        mesh=mesh,
        in_specs=placed,
        out_specs=P(None, "lev", "lat", None),
        check_vma=False,
    )
```

```python
import jax
import jax.numpy as jnp
from jax import lax
from jax.experimental import pallas as pl
from jax.experimental.pallas import tpu as pltpu
from jax.sharding import PartitionSpec as P


NB = 8
F32 = jnp.float32
BF16 = jnp.bfloat16
VM = pltpu.VMEM


def whole():
    return pl.BlockSpec(memory_space=VM)


def in_hbm(array):
    return pltpu.with_memory_space_constraint(array, pltpu.HBM)


def cost(flops, moved):
    return pl.CostEstimate(flops=flops, bytes_accessed=moved, transcendentals=0)


def params(mib):
    return pltpu.CompilerParams(vmem_limit_bytes=mib * 2**20)


def even_band():
    return lax.rem(lax.axis_index("lat"), 2) == 0


def load_kernel(
    state_ref, east_ref, north_ref, weight_ref, list_ref,
    cells_ref, easterly_ref, northerly_ref, weight_out, list_out, near_ref, far_ref, sems,
):
    fields, rows = state_ref.shape[:2]
    last = rows - 1

    def bring(source, target, k):
        copy = pltpu.make_async_copy(source, target, sems.at[k])
        copy.start()
        return copy

    first = [
        bring(state_ref.at[:, last], cells_ref.at[:, last], 0),
        bring(north_ref.at[last], northerly_ref.at[last], 1),
        bring(state_ref.at[:, 0], cells_ref.at[:, 0], 2),
        bring(north_ref.at[:last], northerly_ref.at[:last], 4),
    ]
    rest = [
        bring(state_ref.at[:, 1:last], cells_ref.at[:, 1:last], 3),
        bring(east_ref, easterly_ref, 5),
        bring(weight_ref, weight_out, 6),
        bring(list_ref, list_out, 7),
    ]
    for copy in first:
        copy.wait()
    near_row = jnp.where(even_band(), last, 0)
    for edge_ref, row in ((near_ref, near_row), (far_ref, last - near_row)):
        for f in range(fields):
            edge_ref[f] = cells_ref[f, row].astype(BF16)
        edge_ref[fields] = northerly_ref[row].astype(BF16)
    for copy in rest:
        copy.wait()


def pair_remap(weight):
    n = weight.shape[0]
    row = lax.broadcasted_iota(jnp.int32, (n, n), 0)
    col = lax.broadcasted_iota(jnp.int32, (n, n), 1)
    raw = weight + jnp.where(row == col, 16.0, 0.0)
    remap = (raw / jnp.sum(raw, axis=1, keepdims=True)).T
    zero = jnp.zeros((8, n), F32)
    rows = []
    for m in range(n // 8):
        piece = remap[m * 8 : (m + 1) * 8]
        rows.append(jnp.concatenate([piece, zero], axis=1))
        rows.append(jnp.concatenate([zero, piece], axis=1))
    return jnp.concatenate(rows, axis=0)


def local_kernel(
    state_ref, east_ref, north_ref, list_ref, count_ref, weight_ref,
    out_ref, high_ref, low_ref, mask_ref,
):
    fields, rows, _, width = state_ref.shape
    for f in range(fields):
        below_flux = None
        for j in range(rows):
            cells = state_ref[f, j]
            wind = north_ref[j]
            easterly = east_ref[j]
            east_cells = pltpu.roll(cells, width - 1, 1)
            east_flux = jnp.maximum(easterly, 0.0) * cells + jnp.minimum(easterly, 0.0) * east_cells
            west_flux = pltpu.roll(east_flux, 1, 1)
            value = cells - (east_flux - west_flux)
            if below_flux is not None:
                value = value + below_flux
            if j < rows - 1:
                below_flux = jnp.maximum(wind, 0.0) * cells + jnp.minimum(wind, 0.0) * state_ref[f, j + 1]
                value = value - below_flux
            out_ref[f, j] = value
    pair = pair_remap(weight_ref[...])
    high = pair.astype(BF16)
    high_ref[...] = high
    low_ref[...] = (pair - high.astype(F32)).astype(BF16)
    odd = lax.rem(lax.axis_index("lev"), 2)
    place = lax.broadcasted_iota(jnp.int32, mask_ref.shape, 0)
    column = jnp.where(place < 128, place + 64 * odd, place - 128 * odd)
    block = jnp.right_shift(column * 2731, 16)
    count = count_ref[0, 0]
    active = jnp.zeros(mask_ref.shape, F32)
    for s in range(NB):
        listed = jnp.where(s < count, list_ref[0, :, s : s + 1], -1)
        active = jnp.where(block == listed, 1.0, active)
    mask_ref[...] = active


def finish_kernel(local_ref, state_ref, north_ref, near_ref, far_ref, out_ref):
    fields, rows = state_ref.shape[:2]
    last = rows - 1
    wall = lax.axis_index("lat") == lax.axis_size("lat") - 1
    wind = north_ref[last] * jnp.where(wall, 0.0, 1.0).astype(F32)
    even = even_band()

    def edge(first, second, f):
        return jnp.where(even, first[f].astype(F32), second[f].astype(F32))

    wind_below = edge(far_ref, near_ref, fields)
    rising, sinking = jnp.maximum(wind, 0.0), jnp.minimum(wind, 0.0)
    rising_below, sinking_below = jnp.maximum(wind_below, 0.0), jnp.minimum(wind_below, 0.0)
    low = lax.broadcasted_iota(jnp.int32, (8, 128), 1) < 64
    updated = []
    for f in range(fields):
        south = rising_below * edge(far_ref, near_ref, f) + sinking_below * state_ref[f, 0]
        north = rising * state_ref[f, last] + sinking * edge(near_ref, far_ref, f)
        pieces = [local_ref[f, j] for j in range(rows)]
        pieces[0] = pieces[0] + south
        pieces[last] = pieces[last] - north
        updated.append(pieces)

    def tile(f, v):
        j, k = divmod(v, 8)
        return updated[f][j][:, k * 128 : (k + 1) * 128]

    for p in range(8):
        full_a = [tile(f, 3 * p) for f in range(fields)]
        half = [tile(f, 3 * p + 1) for f in range(fields)]
        full_b = [tile(f, 3 * p + 2) for f in range(fields)]
        turned = [pltpu.roll(h, 64, 1) for h in half]
        half_a = [jnp.where(low, half[f], turned[f + 2]) for f in range(2)]
        half_b = [jnp.where(low, turned[f], half[f + 2]) for f in range(2)]
        out_ref[2 * p] = jnp.concatenate(full_a + half_a, axis=0).astype(BF16)
        out_ref[2 * p + 1] = jnp.concatenate(full_b + half_b, axis=0).astype(BF16)


def silu(v):
    return v / (1.0 + jnp.exp(-v))


def physics_kernel(
    data_ref, high_ref, low_ref, mask_ref, w_in_ref, w_mid_ref, w_out_ref, out_ref
):
    def turned(r):
        block = data_ref[:, r : r + 16, :].reshape(256, 128)
        return block.T

    ends = turned(32)
    x = []
    for p in range(2):
        cols = jnp.concatenate([turned(16 * p), ends[64 * p : 64 * p + 64]], axis=0)
        x.append(
            jnp.dot(cols, high_ref[...], preferred_element_type=F32)
            + jnp.dot(cols, low_ref[...], preferred_element_type=F32)
        )
    remapped = jnp.concatenate(x, axis=1)
    first = silu(jnp.dot(remapped.astype(BF16), w_in_ref[...], preferred_element_type=F32)).astype(BF16)
    second = silu(jnp.dot(first, w_mid_ref[...], preferred_element_type=F32)).astype(BF16)
    tendency = jnp.dot(second, w_out_ref[...], preferred_element_type=F32)
    active = jnp.concatenate([mask_ref[...]] * 4, axis=1) > 0.0
    finished = remapped + jnp.where(active, tendency, 0.0)

    def put(r, rows):
        back = rows.T.reshape(2, 16, 8, 128)
        both = jnp.concatenate([back[0], back[1]], axis=1)
        out_ref[:, r : r + 16, :] = both.astype(BF16)

    put(0, finished[:128, :256])
    put(16, finished[:128, 256:])
    put(32, jnp.concatenate([finished[128:, :256], finished[128:, 256:]], axis=0))


def unpack_kernel(data_ref, out_ref):
    lane = lax.broadcasted_iota(jnp.int32, (16, 128), 1)
    low = lane < 64

    def put(v, pair, value):
        j, k = divmod(v, 8)
        for f in range(2):
            out_ref[2 * pair + f, j, :, k * 128 : (k + 1) * 128] = value[8 * f : 8 * f + 8]

    for p in range(8):
        a = data_ref[2 * p].astype(F32)
        b = data_ref[2 * p + 1].astype(F32)
        for pair in range(2):
            put(3 * p, pair, a[16 * pair : 16 * pair + 16])
            put(3 * p + 2, pair, b[16 * pair : 16 * pair + 16])
        end_a, end_b = a[32:], b[32:]
        put(3 * p + 1, 0, jnp.where(low, end_a, pltpu.roll(end_b, 64, 1)))
        put(3 * p + 1, 1, jnp.where(low, pltpu.roll(end_a, 64, 1), end_b))


def pairs(start, count):
    lower = range(start, count - 1, 2)
    return [(i, i + 1) for i in lower] + [(i + 1, i) for i in lower]


def per_device(
    state, wind_east, wind_north, remap_weight, block_list, block_count, w_in, w_mid, w_out
):
    fields, lev_dev, lat_rows, lon_cells = state.shape
    lev_count = lax.axis_size("lev")
    lat_count = lax.axis_size("lat")
    cells = jnp.transpose(state, (0, 2, 1, 3))
    east = jnp.transpose(wind_east, (1, 0, 2))
    north = jnp.transpose(wind_north, (1, 0, 2))
    edge = (lev_dev, lon_cells)
    smem = pl.BlockSpec(memory_space=pltpu.SMEM)
    hbm = pl.BlockSpec(memory_space=pltpu.HBM)
    levels = lev_dev * lev_count
    col_count = lat_rows * lon_cells // lev_count
    held_cells, held_east, held_north, held_weight, held_list, near, far = pl.pallas_call(
        load_kernel,
        out_shape=[
            jax.ShapeDtypeStruct(cells.shape, F32),
            jax.ShapeDtypeStruct(east.shape, F32),
            jax.ShapeDtypeStruct(north.shape, F32),
            jax.ShapeDtypeStruct(remap_weight.shape, F32),
            jax.ShapeDtypeStruct(block_list.shape, jnp.int32),
            jax.ShapeDtypeStruct((fields + 1, *edge), BF16),
            jax.ShapeDtypeStruct((fields + 1, *edge), BF16),
        ],
        in_specs=[hbm] * 5,
        out_specs=[whole()] * 7,
        scratch_shapes=[pltpu.SemaphoreType.DMA((8,))],
        compiler_params=params(4),
        cost_estimate=cost(1 << 17, 1 << 21),
        name="load",
    )(*map(in_hbm, (cells, east, north, remap_weight, block_list)))
    far = lax.ppermute(far, "lat", pairs(1, lat_count))
    near = lax.ppermute(near, "lat", pairs(0, lat_count))
    local, high, low, mask = pl.pallas_call(
        local_kernel,
        out_shape=[
            jax.ShapeDtypeStruct(cells.shape, F32),
            jax.ShapeDtypeStruct((2 * levels, 2 * levels), BF16),
            jax.ShapeDtypeStruct((2 * levels, 2 * levels), BF16),
            jax.ShapeDtypeStruct((col_count, 128), F32),
        ],
        in_specs=[whole()] * 4 + [smem, whole()],
        out_specs=[whole()] * 4,
        compiler_params=params(4),
        cost_estimate=cost(1 << 22, 1 << 22),
        name="local",
    )(held_cells, held_east, held_north, held_list, block_count, held_weight)
    chunk = (lev_count, fields * lev_dev * lat_rows * lon_cells // lev_count // 128, 128)
    packed = pl.pallas_call(
        finish_kernel,
        out_shape=jax.ShapeDtypeStruct(chunk, BF16),
        in_specs=[whole()] * 5,
        out_specs=whole(),
        compiler_params=params(4),
        cost_estimate=cost(1 << 34, 1 << 20),
        name="finish",
    )(local, held_cells, held_north, near, far)
    packed, high, low, mask = lax.optimization_barrier((packed, high, low, mask))
    columns = lax.all_to_all(packed, "lev", split_axis=0, concat_axis=0, tiled=True)
    finished = pl.pallas_call(
        physics_kernel,
        out_shape=jax.ShapeDtypeStruct(chunk, BF16),
        in_specs=[whole()] * 7,
        out_specs=whole(),
        compiler_params=params(16),
        cost_estimate=cost(1 << 30, 1 << 22),
        name="physics",
    )(columns, high, low, mask, w_in, w_mid, w_out)
    returned = lax.all_to_all(finished, "lev", split_axis=0, concat_axis=0, tiled=True)
    result = pl.pallas_call(
        unpack_kernel,
        out_shape=jax.ShapeDtypeStruct(cells.shape, F32),
        in_specs=[whole()],
        out_specs=whole(),
        compiler_params=params(4),
        cost_estimate=cost(1 << 18, 1 << 20),
        name="unpack",
    )(returned)
    return jnp.transpose(result, (0, 2, 1, 3))


def solution(mesh):
    placed = (
        P(None, "lev", "lat", None),
        P("lev", "lat", None),
        P("lev", "lat", None),
        P(),
        P("lev", "lat", None),
        P("lev", "lat"),
        P(),
        P(),
        P(),
    )
    return jax.shard_map(
        per_device,
        mesh=mesh,
        in_specs=placed,
        out_specs=P(None, "lev", "lat", None),
        check_vma=False,
    )
```

```python
import jax
import jax.numpy as jnp
from jax import lax
from jax.experimental import pallas as pl
from jax.experimental.pallas import tpu as pltpu
from jax.sharding import PartitionSpec as P


NB = 8
F32 = jnp.float32
BF16 = jnp.bfloat16
VM = pltpu.VMEM


def whole():
    return pl.BlockSpec(memory_space=VM)


def in_hbm(array):
    return pltpu.with_memory_space_constraint(array, pltpu.HBM)


def cost(flops, moved):
    return pl.CostEstimate(flops=flops, bytes_accessed=moved, transcendentals=0)


def params(mib):
    return pltpu.CompilerParams(vmem_limit_bytes=mib * 2**20)


def even_band():
    return lax.rem(lax.axis_index("lat"), 2) == 0


def edge_kernel(state_ref, north_ref, near_ref, far_ref, rows_ref, winds_ref, sems):
    fields, rows = state_ref.shape[:2]
    last = rows - 1
    even = even_band()
    near_row = jnp.where(even, last, 0)
    copies = []
    for k, row in enumerate((last - near_row, near_row)):
        for source, target, sem in (
            (state_ref.at[:, row], rows_ref.at[k], sems.at[k, 0]),
            (north_ref.at[row], winds_ref.at[k], sems.at[k, 1]),
        ):
            copy = pltpu.make_async_copy(source, target, sem)
            copy.start()
            copies.append(copy)
    for copy in copies:
        copy.wait()
    for k, edge_ref in enumerate((far_ref, near_ref)):
        for f in range(fields):
            edge_ref[f] = rows_ref[k, f].astype(BF16)
        edge_ref[fields] = winds_ref[k].astype(BF16)


def pair_remap(weight):
    n = weight.shape[0]
    row = lax.broadcasted_iota(jnp.int32, (n, n), 0)
    col = lax.broadcasted_iota(jnp.int32, (n, n), 1)
    raw = weight + jnp.where(row == col, 16.0, 0.0)
    remap = (raw / jnp.sum(raw, axis=1, keepdims=True)).T
    zero = jnp.zeros((8, n), F32)
    rows = []
    for m in range(n // 8):
        piece = remap[m * 8 : (m + 1) * 8]
        rows.append(jnp.concatenate([piece, zero], axis=1))
        rows.append(jnp.concatenate([zero, piece], axis=1))
    return jnp.concatenate(rows, axis=0)


def local_kernel(
    state_ref, east_ref, north_ref, list_ref, count_ref, weight_ref,
    out_ref, high_ref, low_ref, mask_ref,
):
    fields, rows, _, width = state_ref.shape
    for f in range(fields):
        below_flux = None
        for j in range(rows):
            cells = state_ref[f, j]
            wind = north_ref[j]
            easterly = east_ref[j]
            east_cells = pltpu.roll(cells, width - 1, 1)
            east_flux = jnp.maximum(easterly, 0.0) * cells + jnp.minimum(easterly, 0.0) * east_cells
            west_flux = pltpu.roll(east_flux, 1, 1)
            value = cells - (east_flux - west_flux)
            if below_flux is not None:
                value = value + below_flux
            if j < rows - 1:
                below_flux = jnp.maximum(wind, 0.0) * cells + jnp.minimum(wind, 0.0) * state_ref[f, j + 1]
                value = value - below_flux
            out_ref[f, j] = value
    pair = pair_remap(weight_ref[...])
    high = pair.astype(BF16)
    high_ref[...] = high
    low_ref[...] = (pair - high.astype(F32)).astype(BF16)
    odd = lax.rem(lax.axis_index("lev"), 2)
    place = lax.broadcasted_iota(jnp.int32, mask_ref.shape, 0)
    column = jnp.where(place < 128, place + 64 * odd, place - 128 * odd)
    block = jnp.right_shift(column * 2731, 16)
    count = count_ref[0, 0]
    active = jnp.zeros(mask_ref.shape, F32)
    for s in range(NB):
        listed = jnp.where(s < count, list_ref[0, :, s : s + 1], -1)
        active = jnp.where(block == listed, 1.0, active)
    mask_ref[...] = active


def finish_kernel(local_ref, state_ref, north_ref, near_ref, far_ref, out_ref):
    fields, rows = state_ref.shape[:2]
    last = rows - 1
    wall = lax.axis_index("lat") == lax.axis_size("lat") - 1
    wind = north_ref[last] * jnp.where(wall, 0.0, 1.0).astype(F32)
    even = even_band()

    def edge(first, second, f):
        return jnp.where(even, first[f].astype(F32), second[f].astype(F32))

    wind_below = edge(far_ref, near_ref, fields)
    rising, sinking = jnp.maximum(wind, 0.0), jnp.minimum(wind, 0.0)
    rising_below, sinking_below = jnp.maximum(wind_below, 0.0), jnp.minimum(wind_below, 0.0)
    low = lax.broadcasted_iota(jnp.int32, (8, 128), 1) < 64
    updated = []
    for f in range(fields):
        south = rising_below * edge(far_ref, near_ref, f) + sinking_below * state_ref[f, 0]
        north = rising * state_ref[f, last] + sinking * edge(near_ref, far_ref, f)
        pieces = [local_ref[f, j] for j in range(rows)]
        pieces[0] = pieces[0] + south
        pieces[last] = pieces[last] - north
        updated.append(pieces)

    def tile(f, v):
        j, k = divmod(v, 8)
        return updated[f][j][:, k * 128 : (k + 1) * 128]

    for p in range(8):
        full_a = [tile(f, 3 * p) for f in range(fields)]
        half = [tile(f, 3 * p + 1) for f in range(fields)]
        full_b = [tile(f, 3 * p + 2) for f in range(fields)]
        turned = [pltpu.roll(h, 64, 1) for h in half]
        half_a = [jnp.where(low, half[f], turned[f + 2]) for f in range(2)]
        half_b = [jnp.where(low, turned[f], half[f + 2]) for f in range(2)]
        out_ref[2 * p] = jnp.concatenate(full_a + half_a, axis=0).astype(BF16)
        out_ref[2 * p + 1] = jnp.concatenate(full_b + half_b, axis=0).astype(BF16)


def silu(v):
    return v / (1.0 + jnp.exp(-v))


def physics_kernel(
    data_ref, high_ref, low_ref, mask_ref, w_in_ref, w_mid_ref, w_out_ref, out_ref
):
    def turned(r):
        block = data_ref[:, r : r + 16, :].reshape(256, 128)
        return block.T

    ends = turned(32)
    x = []
    for p in range(2):
        cols = jnp.concatenate([turned(16 * p), ends[64 * p : 64 * p + 64]], axis=0)
        x.append(
            jnp.dot(cols, high_ref[...], preferred_element_type=F32)
            + jnp.dot(cols, low_ref[...], preferred_element_type=F32)
        )
    remapped = jnp.concatenate(x, axis=1)
    first = silu(jnp.dot(remapped.astype(BF16), w_in_ref[...], preferred_element_type=F32)).astype(BF16)
    second = silu(jnp.dot(first, w_mid_ref[...], preferred_element_type=F32)).astype(BF16)
    tendency = jnp.dot(second, w_out_ref[...], preferred_element_type=F32)
    active = jnp.concatenate([mask_ref[...]] * 4, axis=1) > 0.0
    finished = remapped + jnp.where(active, tendency, 0.0)

    def put(r, rows):
        back = rows.T.reshape(2, 16, 8, 128)
        both = jnp.concatenate([back[0], back[1]], axis=1)
        out_ref[:, r : r + 16, :] = both.astype(BF16)

    put(0, finished[:128, :256])
    put(16, finished[:128, 256:])
    put(32, jnp.concatenate([finished[128:, :256], finished[128:, 256:]], axis=0))


def unpack_kernel(data_ref, out_ref, buffer, sems):
    fields = out_ref.shape[0]
    low = lax.broadcasted_iota(jnp.int32, (16, 128), 1) < 64
    copies = []
    for pair in range(fields // 2):

        def put(v, value):
            j, k = divmod(v, 8)
            for f in range(2):
                buffer[2 * pair + f, j, :, k * 128 : (k + 1) * 128] = value[8 * f : 8 * f + 8]

        for p in range(8):
            put(3 * p, data_ref[2 * p, 16 * pair : 16 * pair + 16].astype(F32))
            put(3 * p + 2, data_ref[2 * p + 1, 16 * pair : 16 * pair + 16].astype(F32))
            end_a, end_b = (data_ref[2 * p + i, 32:].astype(F32) for i in range(2))
            if pair == 0:
                put(3 * p + 1, jnp.where(low, end_a, pltpu.roll(end_b, 64, 1)))
            else:
                put(3 * p + 1, jnp.where(low, pltpu.roll(end_a, 64, 1), end_b))
        ready = pl.ds(2 * pair, 2)
        copy = pltpu.make_async_copy(buffer.at[ready], out_ref.at[ready], sems.at[pair])
        copy.start()
        copies.append(copy)
    for copy in copies:
        copy.wait()


def pairs(start, count):
    lower = range(start, count - 1, 2)
    return [(i, i + 1) for i in lower] + [(i + 1, i) for i in lower]


def per_device(
    state, wind_east, wind_north, remap_weight, block_list, block_count, w_in, w_mid, w_out
):
    fields, lev_dev, lat_rows, lon_cells = state.shape
    lev_count = lax.axis_size("lev")
    lat_count = lax.axis_size("lat")
    cells = jnp.transpose(state, (0, 2, 1, 3))
    east = jnp.transpose(wind_east, (1, 0, 2))
    north = jnp.transpose(wind_north, (1, 0, 2))
    edge = (lev_dev, lon_cells)
    smem = pl.BlockSpec(memory_space=pltpu.SMEM)
    hbm = pl.BlockSpec(memory_space=pltpu.HBM)
    levels = lev_dev * lev_count
    col_count = lat_rows * lon_cells // lev_count
    near, far = pl.pallas_call(
        edge_kernel,
        out_shape=[jax.ShapeDtypeStruct((fields + 1, *edge), BF16)] * 2,
        in_specs=[hbm] * 2,
        out_specs=[whole()] * 2,
        scratch_shapes=[
            VM((2, fields, *edge), F32),
            VM((2, *edge), F32),
            pltpu.SemaphoreType.DMA((2, 2)),
        ],
        compiler_params=params(4),
        cost_estimate=cost(1 << 33, 1 << 21),
        name="edges",
    )(*map(in_hbm, (cells, north)))
    far = lax.ppermute(far, "lat", pairs(1, lat_count))
    near = lax.ppermute(near, "lat", pairs(0, lat_count))
    local, high, low, mask = pl.pallas_call(
        local_kernel,
        out_shape=[
            jax.ShapeDtypeStruct(cells.shape, F32),
            jax.ShapeDtypeStruct((2 * levels, 2 * levels), BF16),
            jax.ShapeDtypeStruct((2 * levels, 2 * levels), BF16),
            jax.ShapeDtypeStruct((col_count, 128), F32),
        ],
        in_specs=[whole()] * 4 + [smem, whole()],
        out_specs=[whole()] * 4,
        compiler_params=params(4),
        cost_estimate=cost(1 << 22, 1 << 22),
        name="local",
    )(cells, east, north, block_list, block_count, remap_weight)
    chunk = (lev_count, fields * lev_dev * lat_rows * lon_cells // lev_count // 128, 128)
    packed = pl.pallas_call(
        finish_kernel,
        out_shape=jax.ShapeDtypeStruct(chunk, BF16),
        in_specs=[whole()] * 5,
        out_specs=whole(),
        compiler_params=params(4),
        cost_estimate=cost(1 << 34, 1 << 20),
        name="finish",
    )(local, cells, north, near, far)
    packed, high, low, mask = lax.optimization_barrier((packed, high, low, mask))
    columns = lax.all_to_all(packed, "lev", split_axis=0, concat_axis=0, tiled=True)
    finished = pl.pallas_call(
        physics_kernel,
        out_shape=jax.ShapeDtypeStruct(chunk, BF16),
        in_specs=[whole()] * 7,
        out_specs=whole(),
        compiler_params=params(16),
        cost_estimate=cost(1 << 30, 1 << 22),
        name="physics",
    )(columns, high, low, mask, w_in, w_mid, w_out)
    returned = lax.all_to_all(finished, "lev", split_axis=0, concat_axis=0, tiled=True)
    result = pl.pallas_call(
        unpack_kernel,
        out_shape=jax.ShapeDtypeStruct(cells.shape, F32),
        in_specs=[whole()],
        out_specs=hbm,
        scratch_shapes=[VM(cells.shape, F32), pltpu.SemaphoreType.DMA((2,))],
        compiler_params=params(4),
        cost_estimate=cost(1 << 18, 1 << 20),
        name="unpack",
    )(returned)
    return jnp.transpose(result, (0, 2, 1, 3))


def solution(mesh):
    placed = (
        P(None, "lev", "lat", None),
        P("lev", "lat", None),
        P("lev", "lat", None),
        P(),
        P("lev", "lat", None),
        P("lev", "lat"),
        P(),
        P(),
        P(),
    )
    return jax.shard_map(
        per_device,
        mesh=mesh,
        in_specs=placed,
        out_specs=P(None, "lev", "lat", None),
        check_vma=False,
    )
```

```python
import jax
import jax.numpy as jnp
from jax import lax
from jax.experimental import pallas as pl
from jax.experimental.pallas import tpu as pltpu
from jax.sharding import PartitionSpec as P


F32 = jnp.float32
BF16 = jnp.bfloat16
VM = pltpu.VMEM


def whole():
    return pl.BlockSpec(memory_space=VM)


def in_hbm(array):
    return pltpu.with_memory_space_constraint(array, pltpu.HBM)


def cost(flops, moved):
    return pl.CostEstimate(flops=flops, bytes_accessed=moved, transcendentals=0)


def params(mib):
    return pltpu.CompilerParams(vmem_limit_bytes=mib * 2**20)


def even_band():
    return lax.rem(lax.axis_index("lat"), 2) == 0


def edge_kernel(state_ref, north_ref, near_ref, far_ref, rows_ref, winds_ref, sems):
    fields, rows = state_ref.shape[:2]
    last = rows - 1
    even = even_band()
    near_row = jnp.where(even, last, 0)
    copies = []
    for k, row in enumerate((last - near_row, near_row)):
        for source, target, sem in (
            (state_ref.at[:, row], rows_ref.at[k], sems.at[k, 0]),
            (north_ref.at[row], winds_ref.at[k], sems.at[k, 1]),
        ):
            copy = pltpu.make_async_copy(source, target, sem)
            copy.start()
            copies.append(copy)
    for copy in copies:
        copy.wait()
    for k, edge_ref in enumerate((far_ref, near_ref)):
        for f in range(fields):
            edge_ref[f] = rows_ref[k, f].astype(BF16)
        edge_ref[fields] = winds_ref[k].astype(BF16)


def pair_remap(weight):
    n = weight.shape[0]
    row = lax.broadcasted_iota(jnp.int32, (n, n), 0)
    col = lax.broadcasted_iota(jnp.int32, (n, n), 1)
    raw = weight + jnp.where(row == col, 16.0, 0.0)
    remap = (raw / jnp.sum(raw, axis=1, keepdims=True)).T
    zero = jnp.zeros((8, n), F32)
    rows = []
    for m in range(n // 8):
        piece = remap[m * 8 : (m + 1) * 8]
        rows.append(jnp.concatenate([piece, zero], axis=1))
        rows.append(jnp.concatenate([zero, piece], axis=1))
    return jnp.concatenate(rows, axis=0)


def upwind(wind, cells, beyond):
    return wind * jnp.where(wind > 0.0, cells, beyond)


def local_kernel(
    state_ref, east_ref, north_ref, list_ref, count_ref, weight_ref,
    out_ref, high_ref, low_ref, mask_ref,
):
    fields, rows, _, width = state_ref.shape

    def field(f, carry):
        below_flux = None
        for j in range(rows):
            cells = state_ref[f, j]
            wind = north_ref[j]
            easterly = east_ref[j]
            east_cells = pltpu.roll(cells, width - 1, 1)
            east_flux = upwind(easterly, cells, east_cells)
            west_flux = pltpu.roll(east_flux, 1, 1)
            value = cells - (east_flux - west_flux)
            if below_flux is not None:
                value = value + below_flux
            if j < rows - 1:
                below_flux = upwind(wind, cells, state_ref[f, j + 1])
                value = value - below_flux
            out_ref[f, j] = value
        return carry

    lax.fori_loop(0, fields, field, 0)
    pair = pair_remap(weight_ref[...])
    high = pair.astype(BF16)
    high_ref[...] = high
    low_ref[...] = (pair - high.astype(F32)).astype(BF16)
    odd = lax.rem(lax.axis_index("lev"), 2)
    place = lax.broadcasted_iota(jnp.int32, mask_ref.shape, 0)
    column = jnp.where(place < 128, place + 64 * odd, place - 128 * odd)
    block = jnp.right_shift(column * 2731, 16)
    names = list_ref[0]
    slot = lax.broadcasted_iota(jnp.int32, names.shape, 1)
    marks = jnp.where(slot < count_ref[:, :1], jnp.left_shift(jnp.int32(1), names), 0)
    bits = jnp.sum(marks.astype(F32), axis=1, keepdims=True).astype(jnp.int32)
    active = jnp.bitwise_and(jnp.right_shift(bits, block), 1).astype(F32)
    mask_ref[...] = active


def finish_kernel(local_ref, state_ref, north_ref, near_ref, far_ref, out_ref):
    fields, rows = state_ref.shape[:2]
    last = rows - 1
    wall = lax.axis_index("lat") == lax.axis_size("lat") - 1
    wind = north_ref[last] * jnp.where(wall, 0.0, 1.0).astype(F32)
    even = even_band()

    def edge(first, second, f):
        return jnp.where(even, first[f].astype(F32), second[f].astype(F32))

    wind_below = edge(far_ref, near_ref, fields)
    low = lax.broadcasted_iota(jnp.int32, (8, 128), 1) < 64
    updated = []
    for f in range(fields):
        south = upwind(wind_below, edge(far_ref, near_ref, f), state_ref[f, 0])
        north = upwind(wind, state_ref[f, last], edge(near_ref, far_ref, f))
        pieces = [local_ref[f, j] for j in range(rows)]
        pieces[0] = pieces[0] + south
        pieces[last] = pieces[last] - north
        updated.append(pieces)

    def tile(f, v):
        j, k = divmod(v, 8)
        return updated[f][j][:, k * 128 : (k + 1) * 128]

    for p in range(8):
        full_a = [tile(f, 3 * p) for f in range(fields)]
        half = [tile(f, 3 * p + 1) for f in range(fields)]
        full_b = [tile(f, 3 * p + 2) for f in range(fields)]
        turned = [pltpu.roll(h, 64, 1) for h in half]
        half_a = [jnp.where(low, half[f], turned[f + 2]) for f in range(2)]
        half_b = [jnp.where(low, turned[f], half[f + 2]) for f in range(2)]
        out_ref[2 * p] = jnp.concatenate(full_a + half_a, axis=0).astype(BF16)
        out_ref[2 * p + 1] = jnp.concatenate(full_b + half_b, axis=0).astype(BF16)


def silu(v):
    return v / (1.0 + jnp.exp(-v))


def physics_kernel(
    data_ref, high_ref, low_ref, mask_ref, w_in_ref, w_mid_ref, w_out_ref, out_ref
):
    def turned(r):
        block = data_ref[:, r : r + 16, :].reshape(256, 128)
        return block.T

    ends = turned(32)
    x = []
    for p in range(2):
        cols = jnp.concatenate([turned(16 * p), ends[64 * p : 64 * p + 64]], axis=0)
        x.append(
            jnp.dot(cols, high_ref[...], preferred_element_type=F32)
            + jnp.dot(cols, low_ref[...], preferred_element_type=F32)
        )
    remapped = jnp.concatenate(x, axis=1)
    first = silu(jnp.dot(remapped.astype(BF16), w_in_ref[...], preferred_element_type=F32)).astype(BF16)
    second = silu(jnp.dot(first, w_mid_ref[...], preferred_element_type=F32)).astype(BF16)
    tendency = jnp.dot(second, w_out_ref[...], preferred_element_type=F32)
    active = jnp.concatenate([mask_ref[...]] * 4, axis=1) > 0.0
    finished = remapped + jnp.where(active, tendency, 0.0)

    def put(r, rows):
        back = rows.T.reshape(2, 16, 8, 128)
        both = jnp.concatenate([back[0], back[1]], axis=1)
        out_ref[:, r : r + 16, :] = both.astype(BF16)

    put(0, finished[:128, :256])
    put(16, finished[:128, 256:])
    put(32, jnp.concatenate([finished[128:, :256], finished[128:, 256:]], axis=0))


def unpack_kernel(data_ref, out_ref, buffer, sems):
    fields = out_ref.shape[0]
    low = lax.broadcasted_iota(jnp.int32, (16, 128), 1) < 64
    copies = []
    for pair in range(fields // 2):

        def put(v, value):
            j, k = divmod(v, 8)
            for f in range(2):
                buffer[2 * pair + f, j, :, k * 128 : (k + 1) * 128] = value[8 * f : 8 * f + 8]

        for p in range(8):
            put(3 * p, data_ref[2 * p, 16 * pair : 16 * pair + 16].astype(F32))
            put(3 * p + 2, data_ref[2 * p + 1, 16 * pair : 16 * pair + 16].astype(F32))
            end_a, end_b = (data_ref[2 * p + i, 32:].astype(F32) for i in range(2))
            if pair == 0:
                put(3 * p + 1, jnp.where(low, end_a, pltpu.roll(end_b, 64, 1)))
            else:
                put(3 * p + 1, jnp.where(low, pltpu.roll(end_a, 64, 1), end_b))
        ready = pl.ds(2 * pair, 2)
        copy = pltpu.make_async_copy(buffer.at[ready], out_ref.at[ready], sems.at[pair])
        copy.start()
        copies.append(copy)
    for copy in copies:
        copy.wait()


def pairs(start, count):
    lower = range(start, count - 1, 2)
    return [(i, i + 1) for i in lower] + [(i + 1, i) for i in lower]


def per_device(
    state, wind_east, wind_north, remap_weight, block_list, block_count, w_in, w_mid, w_out
):
    fields, lev_dev, lat_rows, lon_cells = state.shape
    lev_count = lax.axis_size("lev")
    lat_count = lax.axis_size("lat")
    cells = jnp.transpose(state, (0, 2, 1, 3))
    east = jnp.transpose(wind_east, (1, 0, 2))
    north = jnp.transpose(wind_north, (1, 0, 2))
    edge = (lev_dev, lon_cells)
    hbm = pl.BlockSpec(memory_space=pltpu.HBM)
    levels = lev_dev * lev_count
    col_count = lat_rows * lon_cells // lev_count
    near, far = pl.pallas_call(
        edge_kernel,
        out_shape=[jax.ShapeDtypeStruct((fields + 1, *edge), BF16)] * 2,
        in_specs=[hbm] * 2,
        out_specs=[whole()] * 2,
        scratch_shapes=[
            VM((2, fields, *edge), F32),
            VM((2, *edge), F32),
            pltpu.SemaphoreType.DMA((2, 2)),
        ],
        compiler_params=params(4),
        cost_estimate=cost(1 << 33, 1 << 21),
        name="edges",
    )(*map(in_hbm, (cells, north)))
    far = lax.ppermute(far, "lat", pairs(1, lat_count))
    near = lax.ppermute(near, "lat", pairs(0, lat_count))
    local, high, low, mask = pl.pallas_call(
        local_kernel,
        out_shape=[
            jax.ShapeDtypeStruct(cells.shape, F32),
            jax.ShapeDtypeStruct((2 * levels, 2 * levels), BF16),
            jax.ShapeDtypeStruct((2 * levels, 2 * levels), BF16),
            jax.ShapeDtypeStruct((col_count, 128), F32),
        ],
        in_specs=[whole()] * 6,
        out_specs=[whole()] * 4,
        compiler_params=params(4),
        cost_estimate=cost(1 << 22, 1 << 22),
        name="local",
    )(cells, east, north, block_list, lax.pad(block_count, jnp.int32(0), ((0, 0, 0), (0, 127, 0))), remap_weight)
    chunk = (lev_count, fields * lev_dev * lat_rows * lon_cells // lev_count // 128, 128)
    packed = pl.pallas_call(
        finish_kernel,
        out_shape=jax.ShapeDtypeStruct(chunk, BF16),
        in_specs=[whole()] * 5,
        out_specs=whole(),
        compiler_params=params(4),
        cost_estimate=cost(1 << 34, 1 << 20),
        name="finish",
    )(local, cells, north, near, far)
    packed, high, low, mask = lax.optimization_barrier((packed, high, low, mask))
    columns = lax.all_to_all(packed, "lev", split_axis=0, concat_axis=0, tiled=True)
    finished = pl.pallas_call(
        physics_kernel,
        out_shape=jax.ShapeDtypeStruct(chunk, BF16),
        in_specs=[whole()] * 7,
        out_specs=whole(),
        compiler_params=params(16),
        cost_estimate=cost(1 << 30, 1 << 22),
        name="physics",
    )(columns, high, low, mask, w_in, w_mid, w_out)
    returned = lax.all_to_all(finished, "lev", split_axis=0, concat_axis=0, tiled=True)
    result = pl.pallas_call(
        unpack_kernel,
        out_shape=jax.ShapeDtypeStruct(cells.shape, F32),
        in_specs=[whole()],
        out_specs=hbm,
        scratch_shapes=[VM(cells.shape, F32), pltpu.SemaphoreType.DMA((2,))],
        compiler_params=params(4),
        cost_estimate=cost(1 << 18, 1 << 20),
        name="unpack",
    )(returned)
    return jnp.transpose(result, (0, 2, 1, 3))


def solution(mesh):
    placed = (
        P(None, "lev", "lat", None),
        P("lev", "lat", None),
        P("lev", "lat", None),
        P(),
        P("lev", "lat", None),
        P("lev", "lat"),
        P(),
        P(),
        P(),
    )
    return jax.shard_map(
        per_device,
        mesh=mesh,
        in_specs=placed,
        out_specs=P(None, "lev", "lat", None),
        check_vma=False,
    )
```

```python
import jax
import jax.numpy as jnp
from jax import lax
from jax.experimental import pallas as pl
from jax.experimental.pallas import tpu as pltpu
from jax.sharding import PartitionSpec as P


F32 = jnp.float32
BF16 = jnp.bfloat16
VM = pltpu.VMEM


def whole():
    return pl.BlockSpec(memory_space=VM)


def in_hbm(array):
    return pltpu.with_memory_space_constraint(array, pltpu.HBM)


def cost(flops, moved):
    return pl.CostEstimate(flops=flops, bytes_accessed=moved, transcendentals=0)


def params(mib):
    return pltpu.CompilerParams(vmem_limit_bytes=mib * 2**20)


def even_band():
    return lax.rem(lax.axis_index("lat"), 2) == 0


def edge_kernel(state_ref, north_ref, near_ref, far_ref, rows_ref, winds_ref, sems):
    fields, rows = state_ref.shape[:2]
    last = rows - 1
    even = even_band()
    near_row = jnp.where(even, last, 0)
    copies = []
    for k, row in enumerate((last - near_row, near_row)):
        for source, target, sem in (
            (state_ref.at[:, row], rows_ref.at[k], sems.at[k, 0]),
            (north_ref.at[row], winds_ref.at[k], sems.at[k, 1]),
        ):
            copy = pltpu.make_async_copy(source, target, sem)
            copy.start()
            copies.append(copy)
    for copy in copies:
        copy.wait()
    for k, edge_ref in enumerate((far_ref, near_ref)):
        for f in range(fields):
            edge_ref[f] = rows_ref[k, f].astype(BF16)
        edge_ref[fields] = winds_ref[k].astype(BF16)


def pair_remap(weight):
    n = weight.shape[0]
    row = lax.broadcasted_iota(jnp.int32, (n, n), 0)
    col = lax.broadcasted_iota(jnp.int32, (n, n), 1)
    raw = weight + jnp.where(row == col, 16.0, 0.0)
    remap = (raw / jnp.sum(raw, axis=1, keepdims=True)).T
    zero = jnp.zeros((8, n), F32)
    rows = []
    for m in range(n // 8):
        piece = remap[m * 8 : (m + 1) * 8]
        rows.append(jnp.concatenate([piece, zero], axis=1))
        rows.append(jnp.concatenate([zero, piece], axis=1))
    return jnp.concatenate(rows, axis=0)


def upwind(wind, cells, beyond):
    return wind * jnp.where(wind > 0.0, cells, beyond)


def local_kernel(
    state_ref, east_ref, north_ref, list_ref, count_ref, weight_ref,
    out_ref, high_ref, low_ref, mask_ref,
):
    fields, rows, _, width = state_ref.shape

    def field(f, carry):
        below_flux = None
        for j in range(rows):
            cells = state_ref[f, j]
            wind = north_ref[j]
            easterly = east_ref[j]
            east_cells = pltpu.roll(cells, width - 1, 1)
            east_flux = upwind(easterly, cells, east_cells)
            west_flux = pltpu.roll(east_flux, 1, 1)
            value = cells - (east_flux - west_flux)
            if below_flux is not None:
                value = value + below_flux
            if j < rows - 1:
                below_flux = upwind(wind, cells, state_ref[f, j + 1])
                value = value - below_flux
            out_ref[f, j] = value
        return carry

    lax.fori_loop(0, fields, field, 0)
    pair = pair_remap(weight_ref[...])
    high = pair.astype(BF16)
    high_ref[...] = high
    low_ref[...] = (pair - high.astype(F32)).astype(BF16)
    odd = lax.rem(lax.axis_index("lev"), 2)
    place = lax.broadcasted_iota(jnp.int32, mask_ref.shape, 0)
    column = jnp.where(place < 128, place + 64 * odd, place - 128 * odd)
    block = jnp.right_shift(column * 2731, 16)
    names = list_ref[0]
    slot = lax.broadcasted_iota(jnp.int32, names.shape, 1)
    marks = jnp.where(slot < count_ref[0, 0], jnp.left_shift(jnp.int32(1), names), 0)
    bits = jnp.sum(marks.astype(F32), axis=1, keepdims=True).astype(jnp.int32)
    active = jnp.bitwise_and(jnp.right_shift(bits, block), 1).astype(F32)
    mask_ref[...] = active


def finish_kernel(local_ref, state_ref, north_ref, near_ref, far_ref, out_ref):
    fields, rows = state_ref.shape[:2]
    last = rows - 1
    wall = lax.axis_index("lat") == lax.axis_size("lat") - 1
    wind = north_ref[last] * jnp.where(wall, 0.0, 1.0).astype(F32)
    even = even_band()

    def edge(first, second, f):
        return jnp.where(even, first[f].astype(F32), second[f].astype(F32))

    wind_below = edge(far_ref, near_ref, fields)
    low = lax.broadcasted_iota(jnp.int32, (8, 128), 1) < 64
    updated = []
    for f in range(fields):
        south = upwind(wind_below, edge(far_ref, near_ref, f), state_ref[f, 0])
        north = upwind(wind, state_ref[f, last], edge(near_ref, far_ref, f))
        pieces = [local_ref[f, j] for j in range(rows)]
        pieces[0] = pieces[0] + south
        pieces[last] = pieces[last] - north
        updated.append(pieces)

    def tile(f, v):
        j, k = divmod(v, 8)
        return updated[f][j][:, k * 128 : (k + 1) * 128]

    for p in range(8):
        full_a = [tile(f, 3 * p) for f in range(fields)]
        half = [tile(f, 3 * p + 1) for f in range(fields)]
        full_b = [tile(f, 3 * p + 2) for f in range(fields)]
        turned = [pltpu.roll(h, 64, 1) for h in half]
        half_a = [jnp.where(low, half[f], turned[f + 2]) for f in range(2)]
        half_b = [jnp.where(low, turned[f], half[f + 2]) for f in range(2)]
        out_ref[2 * p] = jnp.concatenate(full_a + half_a, axis=0).astype(BF16)
        out_ref[2 * p + 1] = jnp.concatenate(full_b + half_b, axis=0).astype(BF16)


def silu(v):
    return v / (1.0 + jnp.exp(-v))


def physics_kernel(
    data_ref, high_ref, low_ref, mask_ref, w_in_ref, w_mid_ref, w_out_ref, out_ref
):
    def turned(r):
        block = data_ref[:, r : r + 16, :].reshape(256, 128)
        return block.T

    ends = turned(32)
    x = []
    for p in range(2):
        cols = jnp.concatenate([turned(16 * p), ends[64 * p : 64 * p + 64]], axis=0)
        x.append(
            jnp.dot(cols, high_ref[...], preferred_element_type=F32)
            + jnp.dot(cols, low_ref[...], preferred_element_type=F32)
        )
    remapped = jnp.concatenate(x, axis=1)
    first = silu(jnp.dot(remapped.astype(BF16), w_in_ref[...], preferred_element_type=F32)).astype(BF16)
    second = silu(jnp.dot(first, w_mid_ref[...], preferred_element_type=F32)).astype(BF16)
    tendency = jnp.dot(second, w_out_ref[...], preferred_element_type=F32)
    active = jnp.concatenate([mask_ref[...]] * 4, axis=1) > 0.0
    finished = remapped + jnp.where(active, tendency, 0.0)

    def put(r, rows):
        back = rows.T.reshape(2, 16, 8, 128)
        both = jnp.concatenate([back[0], back[1]], axis=1)
        out_ref[:, r : r + 16, :] = both.astype(BF16)

    put(0, finished[:128, :256])
    put(16, finished[:128, 256:])
    put(32, jnp.concatenate([finished[128:, :256], finished[128:, 256:]], axis=0))


def unpack_kernel(data_ref, out_ref, buffer, sems):
    fields = out_ref.shape[0]
    low = lax.broadcasted_iota(jnp.int32, (16, 128), 1) < 64
    copies = []
    for pair in range(fields // 2):

        def put(v, value):
            j, k = divmod(v, 8)
            for f in range(2):
                buffer[2 * pair + f, j, :, k * 128 : (k + 1) * 128] = value[8 * f : 8 * f + 8]

        for p in range(8):
            put(3 * p, data_ref[2 * p, 16 * pair : 16 * pair + 16].astype(F32))
            put(3 * p + 2, data_ref[2 * p + 1, 16 * pair : 16 * pair + 16].astype(F32))
            end_a, end_b = (data_ref[2 * p + i, 32:].astype(F32) for i in range(2))
            if pair == 0:
                put(3 * p + 1, jnp.where(low, end_a, pltpu.roll(end_b, 64, 1)))
            else:
                put(3 * p + 1, jnp.where(low, pltpu.roll(end_a, 64, 1), end_b))
        ready = pl.ds(2 * pair, 2)
        copy = pltpu.make_async_copy(buffer.at[ready], out_ref.at[ready], sems.at[pair])
        copy.start()
        copies.append(copy)
    for copy in copies:
        copy.wait()


def pairs(start, count):
    lower = range(start, count - 1, 2)
    return [(i, i + 1) for i in lower] + [(i + 1, i) for i in lower]


def per_device(
    state, wind_east, wind_north, remap_weight, block_list, block_count, w_in, w_mid, w_out
):
    fields, lev_dev, lat_rows, lon_cells = state.shape
    lev_count = lax.axis_size("lev")
    lat_count = lax.axis_size("lat")
    cells = jnp.transpose(state, (0, 2, 1, 3))
    east = jnp.transpose(wind_east, (1, 0, 2))
    north = jnp.transpose(wind_north, (1, 0, 2))
    edge = (lev_dev, lon_cells)
    smem = pl.BlockSpec(memory_space=pltpu.SMEM)
    hbm = pl.BlockSpec(memory_space=pltpu.HBM)
    levels = lev_dev * lev_count
    col_count = lat_rows * lon_cells // lev_count
    near, far = pl.pallas_call(
        edge_kernel,
        out_shape=[jax.ShapeDtypeStruct((fields + 1, *edge), BF16)] * 2,
        in_specs=[hbm] * 2,
        out_specs=[whole()] * 2,
        scratch_shapes=[
            VM((2, fields, *edge), F32),
            VM((2, *edge), F32),
            pltpu.SemaphoreType.DMA((2, 2)),
        ],
        compiler_params=params(4),
        cost_estimate=cost(1 << 33, 1 << 21),
        name="edges",
    )(*map(in_hbm, (cells, north)))
    far = lax.ppermute(far, "lat", pairs(1, lat_count))
    near = lax.ppermute(near, "lat", pairs(0, lat_count))
    local, high, low, mask = pl.pallas_call(
        local_kernel,
        out_shape=[
            jax.ShapeDtypeStruct(cells.shape, F32),
            jax.ShapeDtypeStruct((2 * levels, 2 * levels), BF16),
            jax.ShapeDtypeStruct((2 * levels, 2 * levels), BF16),
            jax.ShapeDtypeStruct((col_count, 128), F32),
        ],
        in_specs=[whole()] * 4 + [smem, whole()],
        out_specs=[whole()] * 4,
        compiler_params=params(4),
        cost_estimate=cost(1 << 22, 1 << 22),
        name="local",
    )(cells, east, north, block_list, block_count, remap_weight)
    chunk = (lev_count, fields * lev_dev * lat_rows * lon_cells // lev_count // 128, 128)
    packed = pl.pallas_call(
        finish_kernel,
        out_shape=jax.ShapeDtypeStruct(chunk, BF16),
        in_specs=[whole()] * 5,
        out_specs=whole(),
        compiler_params=params(4),
        cost_estimate=cost(1 << 34, 1 << 20),
        name="finish",
    )(local, cells, north, near, far)
    packed, high, low, mask = lax.optimization_barrier((packed, high, low, mask))
    columns = lax.all_to_all(packed, "lev", split_axis=0, concat_axis=0, tiled=True)
    finished = pl.pallas_call(
        physics_kernel,
        out_shape=jax.ShapeDtypeStruct(chunk, BF16),
        in_specs=[whole()] * 7,
        out_specs=whole(),
        compiler_params=params(16),
        cost_estimate=cost(1 << 30, 1 << 22),
        name="physics",
    )(columns, high, low, mask, w_in, w_mid, w_out)
    returned = lax.all_to_all(finished, "lev", split_axis=0, concat_axis=0, tiled=True)
    result = pl.pallas_call(
        unpack_kernel,
        out_shape=jax.ShapeDtypeStruct(cells.shape, F32),
        in_specs=[whole()],
        out_specs=hbm,
        scratch_shapes=[VM(cells.shape, F32), pltpu.SemaphoreType.DMA((2,))],
        compiler_params=params(4),
        cost_estimate=cost(1 << 18, 1 << 20),
        name="unpack",
    )(returned)
    return jnp.transpose(result, (0, 2, 1, 3))


def solution(mesh):
    placed = (
        P(None, "lev", "lat", None),
        P("lev", "lat", None),
        P("lev", "lat", None),
        P(),
        P("lev", "lat", None),
        P("lev", "lat"),
        P(),
        P(),
        P(),
    )
    return jax.shard_map(
        per_device,
        mesh=mesh,
        in_specs=placed,
        out_specs=P(None, "lev", "lat", None),
        check_vma=False,
    )
```
